128 devices in a mesh: section: 8 (over z_hi, x), seq: 16 (over z_lo, y, core).
Axes of the slice: x: 4, y: 4, z: 4 (z_hi: 2, z_lo: 2; z = z_hi * 2 + z_lo), core: 2. Of those that a mesh axis runs over, the one named last changes fastest.
Arguments:
- grad_out: bfloat16 [8, 2048, 8192], P('section', 'seq'), may hold values from -7.5 to 7.5
- queries: bfloat16 [8, 2048, 8192], P('section', 'seq'), may hold values from -2.5 to 2.5
- mem_out: bfloat16 [8, 2048, 8192], P('section', 'seq'), may hold values from -6 to 6
- row_total: bfloat16 [8, 2048, 64], P('section', 'seq'), may hold values from 8192 to 32768
- gate_logit: float32 [8, 64], P('section'), may hold values from -2 to 2
- mem_keys: bfloat16 [8, 16384, 1024], P('section', 'seq'), may hold values from -3.5 to 3.5
- mem_values: bfloat16 [8, 16384, 1024], P('section', 'seq'), may hold values from -7.5 to 7.5
- retrieved: int32 [8, 8, 16, 32], P('section'), may hold values from 0 to 127, all different within a row
Outputs:
- onward: bfloat16 [8, 2048, 8192], P('section', 'seq')
The draws below stay inside these ranges and needn't reach their ends.
Inputs may be any that keep to these rules, and one draw needn't show every extreme that they name: `retrieved`: 32 different memory blocks for each section, key head and query block; every memory block is named somewhere, some far more often than others.
All inputs are finite; a program needn't handle non-finite values.
Results may differ from the reference program's by a relative error of at most 0.0054.
Values may be sent and summed in bfloat16 or wider, within the bound.
A program may use at most 128 MiB of HBM per device.

```python
import math
import jax
import jax.numpy as jnp
from jax import lax

HEADS = 64
KV_HEADS = 8
HEAD_DIM = 128
TOPK = 32
BLOCK = 128
SECTIONS = 8
TOKENS = 2048
MEM = 16384
QBLOCKS = 16
MBLOCKS = 128
WIDTH = 8192
KV_WIDTH = 1024


def steps_of(rng, shape, split, smallest, largest):
    def one(axis_at, parts):
        steps = jax.random.uniform(jax.random.fold_in(jax.random.fold_in(rng, 6), axis_at), (parts,), jnp.float32, smallest / len(split), largest / len(split))
        return jnp.repeat(jnp.exp(steps), shape[axis_at] // parts).reshape((-1,) + (1,) * (len(shape) - axis_at - 1))

    loudness = one(*split[0])
    for cut in split[1:]:
        loudness = loudness * one(*cut)
    return loudness


def different_ones(stream_key, rows, number_of, top, lift):
    order = jax.random.permutation(jax.random.fold_in(stream_key, 1), number_of)
    boost = order
    for power in range(3):
        boost = boost * boost // number_of
    boost = boost * lift // number_of
    lots = jax.random.randint(jax.random.fold_in(stream_key, 2), (rows, number_of), 0, 4096) + boost
    sure = jax.random.permutation(jax.random.fold_in(stream_key, 3), rows)[jnp.arange(number_of) % rows]
    lots = jnp.where(jnp.arange(rows)[:, None] == sure[None, :], 1 << 14, lots)
    priority = lots * number_of + jnp.arange(number_of)
    return lax.top_k(priority.astype(jnp.int32), top)[1].astype(jnp.int32)


def scatter_about(own_key, dims, scale, reach, shards=(), dtype=jnp.bfloat16):
    values = scale * jax.random.normal(own_key, dims, jnp.float32)
    if shards:
        values = values * steps_of(own_key, dims, shards, -0.22, 0.18)
    return jnp.clip(values, -reach, reach).astype(dtype)


def setup_inputs(seed: int = 0) -> dict:
    keys = jax.random.split(jax.random.key(seed), 9)
    return {
        "grad_out": scatter_about(keys[0], (SECTIONS, TOKENS, WIDTH), 3.0, 7.5, ((0, 8), (1, 16))),
        "queries": scatter_about(keys[1], (SECTIONS, TOKENS, WIDTH), 1.0, 2.5, ((0, 8), (1, 16))),
        "mem_out": scatter_about(keys[2], (SECTIONS, TOKENS, WIDTH), 1.0, 6.0, ((0, 8), (1, 16))),
        "row_total": jnp.clip(jnp.exp(math.log(32768.0) - 1.3862944 * jax.random.uniform(keys[3], (SECTIONS, TOKENS, HEADS), jnp.float32) ** steps_of(keys[3], (SECTIONS, TOKENS, HEADS), ((0, 8), (1, 16)), -0.2, 0.2)), 8192.0, 32768.0).astype(jnp.bfloat16),
        "gate_logit": jnp.clip(jax.random.uniform(keys[4], (SECTIONS, HEADS), jnp.float32, -2.0, 2.0) * steps_of(keys[4], (SECTIONS, HEADS), ((0, 8),), -0.4, 0.0), -2.0, 2.0),
        "mem_keys": scatter_about(keys[5], (SECTIONS, MEM, KV_WIDTH), 1.4, 3.5, ((0, 8), (1, 16))),
        "mem_values": scatter_about(keys[6], (SECTIONS, MEM, KV_WIDTH), 3.0, 7.5, ((0, 8), (1, 16))),
        "retrieved": different_ones(keys[7], SECTIONS * KV_HEADS * QBLOCKS, MBLOCKS, TOPK, 4096).reshape((SECTIONS, KV_HEADS, QBLOCKS, TOPK)),
    }


def reference(grad_out, queries, mem_out, row_total, gate_logit, mem_keys, mem_values, retrieved):
    group_size = HEADS // KV_HEADS
    score_scale = HEAD_DIM ** -0.5

    def one_section(pieces):
        grad_section, query_section, out_section, sum_section, logit_section, keys_section, values_section, chosen = pieces
        gate_values = jax.nn.sigmoid(logit_section.astype(jnp.float32))
        grad_mem = (gate_values[None, :, None] * grad_section.reshape(TOKENS, HEADS, HEAD_DIM).astype(jnp.float32)).astype(jnp.bfloat16)
        row_delta = jnp.sum(grad_mem.astype(jnp.float32) * out_section.reshape(TOKENS, HEADS, HEAD_DIM).astype(jnp.float32), axis=-1)
        key_blocks = keys_section.reshape(MBLOCKS, BLOCK, KV_HEADS, HEAD_DIM).transpose(2, 0, 1, 3)
        value_blocks = values_section.reshape(MBLOCKS, BLOCK, KV_HEADS, HEAD_DIM).transpose(2, 0, 1, 3)

        def one_block(items):
            query_tile, grad_tile, delta_tile, sum_tile, picks = items
            tile_keys = jax.vmap(lambda table, rows_of: table[rows_of].reshape(TOPK * BLOCK, HEAD_DIM))(key_blocks, picks)
            tile_values = jax.vmap(lambda table, rows_of: table[rows_of].reshape(TOPK * BLOCK, HEAD_DIM))(value_blocks, picks)
            query_four = query_tile.reshape(BLOCK, KV_HEADS, group_size, HEAD_DIM).astype(jnp.float32)
            grad_four = grad_tile.reshape(BLOCK, KV_HEADS, group_size, HEAD_DIM).astype(jnp.float32)
            scores = jnp.einsum("qkgd,kjd->qkgj", query_four, tile_keys.astype(jnp.float32)) * score_scale
            probs = jnp.exp(scores - jnp.log(sum_tile.reshape(BLOCK, KV_HEADS, group_size).astype(jnp.float32))[..., None])
            grad_probs = jnp.einsum("qkgd,kjd->qkgj", grad_four, tile_values.astype(jnp.float32))
            grad_scores = (probs * (grad_probs - delta_tile.reshape(BLOCK, KV_HEADS, group_size)[..., None]) * score_scale).astype(jnp.bfloat16)
            result = jnp.einsum("qkgj,kjd->qkgd", grad_scores.astype(jnp.float32), tile_keys.astype(jnp.float32))
            return result.astype(jnp.bfloat16).reshape(BLOCK, WIDTH)

        blocks_in = (
            query_section.reshape(QBLOCKS, BLOCK, HEADS, HEAD_DIM),
            grad_mem.reshape(QBLOCKS, BLOCK, HEADS, HEAD_DIM),
            row_delta.reshape(QBLOCKS, BLOCK, HEADS),
            sum_section.reshape(QBLOCKS, BLOCK, HEADS),
            chosen.transpose(1, 0, 2),
        )
        return lax.map(one_block, blocks_in).reshape(TOKENS, WIDTH)

    grads = lax.map(one_section, (grad_out, queries, mem_out, row_total, gate_logit, mem_keys, mem_values, retrieved))
    return jnp.roll(grads, -1, axis=0)
```

```python
import functools

import jax
import jax.numpy as jnp
from jax import lax
from jax.experimental import pallas as pl
from jax.experimental.pallas import tpu as pltpu
from jax.sharding import PartitionSpec as P

BLOCK = 128
PICKS_A_TILE = 16
LOG2E = 1.4426950408889634
MESH = pl.DeviceIdType.MESH
CONTRACT_LAST = (((1,), (1,)), ((), ()))
CHIP_STEPS = ((1, 0), (0, 1), (0, 3), (1, 1), (0, 2), (1, 3), (1, 2))


def step_offsets(step):
    core = step % 2
    pair = step // 2
    turn = pair // 2
    return pair % 2, turn + (turn // 2) * (1 - 2 * (turn % 2)), core


def kernel(
    sections, members, heads_here, head_dim, picks_count,
    grad_ref, query_ref, out_in_ref, total_ref, gate_ref, key_ref, value_ref, picks_ref,
    result_ref,
    keys, values, head_query, head_grad, row_pack, row_send, gates, done, own_grad, own_out,
    key_send, key_recv, relay_send, relay_recv, token_send, token_recv, out_send, out_recv, local_sem,
):
    section = lax.axis_index("section")
    me = lax.axis_index("seq")
    chips = members // 2
    ring = chips // 2
    core = me % 2
    chip = me // 2
    high = chip // ring
    low = chip % ring
    width = heads_here * head_dim
    blocks_dev = key_ref.shape[0]
    behind = (section + sections - 1) % sections
    ahead = (section + 1) % sections

    def chip_at(dz, dy):
        return ((high + dz) % 2) * ring + (low + dy) % ring

    def member_at(dz, dy, dc):
        return chip_at(dz, dy) * 2 + (core + dc) % 2

    barrier = pltpu.get_barrier_semaphore()

    def greet(i, carry):
        pl.semaphore_signal(barrier, inc=1, device_id=(section, (me + i) % members), device_id_type=MESH)
        return carry

    def greet_sections(i, carry):
        pl.semaphore_signal(barrier, inc=1, device_id=(behind, i), device_id_type=MESH)
        pl.semaphore_signal(barrier, inc=1, device_id=(ahead, i), device_id_type=MESH)
        return carry

    lax.fori_loop(1, members, greet, 0)
    lax.fori_loop(0, members, greet_sections, 0)

    own_copies = [
        pltpu.make_async_copy(grad_ref, own_grad, local_sem.at[0]),
        pltpu.make_async_copy(out_in_ref, own_out, local_sem.at[1]),
    ]
    for copy in own_copies:
        copy.start()
    pl.semaphore_wait(barrier, members - 1 + 2 * members)

    def columns(index, size):
        return pl.ds(pl.multiple_of(index * size, size), size)

    own_rows = pl.ds(me * blocks_dev, blocks_dev)

    sent = []
    for n, (dz, dy) in enumerate(CHIP_STEPS):
        target = chip_at(dz, dy)
        for a, (source, held) in enumerate(((key_ref, keys), (value_ref, values))):
            copy = pltpu.make_async_remote_copy(
                src_ref=source.at[:, :, columns(target, head_dim)],
                dst_ref=held.at[own_rows],
                send_sem=key_send.at[n, a],
                recv_sem=key_recv.at[n, a],
                device_id=(section, target * 2 + core),
                device_id_type=MESH,
            )
            copy.start()
            sent.append(copy)
    partner = (section, chip * 2 + 1 - core)
    relayed, here = [], []
    for a, (source, held) in enumerate(((key_ref, keys), (value_ref, values))):
        mine = source.at[:, :, columns(chip, head_dim)]
        copy = pltpu.make_async_remote_copy(
            src_ref=mine, dst_ref=held.at[own_rows],
            send_sem=relay_send.at[len(CHIP_STEPS), a], recv_sem=relay_recv.at[len(CHIP_STEPS), a],
            device_id=partner, device_id_type=MESH,
        )
        copy.start()
        relayed.append(copy)
        copy = pltpu.make_async_copy(mine, held.at[own_rows], local_sem.at[2 + a])
        copy.start()
        here.append(copy)

    def token_copy(step, a):
        dz, dy, dc = step_offsets(step)
        target = member_at(2 - dz, ring - dy, dc)
        source, held = ((query_ref, head_query), (grad_ref, head_grad))[a]
        return pltpu.make_async_remote_copy(
            src_ref=source.at[:, columns(target, width)],
            dst_ref=held.at[me],
            send_sem=token_send.at[step, a],
            recv_sem=token_recv.at[step, a],
            device_id=(section, target),
            device_id_type=MESH,
        )

    def row_copy(step):
        dz, dy, dc = step_offsets(step)
        target = member_at(2 - dz, ring - dy, dc)
        return pltpu.make_async_remote_copy(
            src_ref=row_send.at[target],
            dst_ref=row_pack.at[me],
            send_sem=token_send.at[step, 2],
            recv_sem=token_recv.at[step, 2],
            device_id=(section, target),
            device_id_type=MESH,
        )

    for step in range(1, members):
        for a in range(2):
            token_copy(step, a).start()
    for a, (source, held) in enumerate(((query_ref, head_query), (grad_ref, head_grad))):
        copy = pltpu.make_async_copy(source.at[:, columns(me, width)], held.at[me], local_sem.at[4 + a])
        copy.start()
        here.append(copy)

    gate_row = 1.0 / (1.0 + jnp.exp(-gate_ref[...]))
    lanes = lax.broadcasted_iota(jnp.int32, gate_row.shape, 1)
    for h in range(heads_here):
        mine = jnp.sum(jnp.where(lanes == me * heads_here + h, gate_row, 0.0), axis=1, keepdims=True)
        gates[h : h + 1, :] = jnp.broadcast_to(mine, (1, head_dim))
    for copy in own_copies:
        copy.wait()
    tokens = own_grad.shape[0]
    log_total = jnp.log2(total_ref[...].astype(jnp.float32)) + 0.5 * 7.0
    lane = lax.broadcasted_iota(jnp.int32, (tokens, 128), 1)
    packed = jnp.zeros((tokens, 128), jnp.float32)
    for h in range(members * heads_here):
        cut = slice(h * head_dim, (h + 1) * head_dim)
        gated = (own_grad[:, cut].astype(jnp.float32) * gate_row[:, h : h + 1]).astype(jnp.bfloat16)
        delta = jnp.sum(gated.astype(jnp.float32) * own_out[:, cut].astype(jnp.float32), axis=1, keepdims=True)
        at = (h // heads_here) * 2 * heads_here + h % heads_here
        packed = jnp.where(lane == at, delta, packed)
        packed = jnp.where(lane == at + heads_here, log_total[:, h : h + 1], packed)
    row_send[...] = packed.T.reshape(row_send.shape)
    row_pack[me] = row_send[me]

    for n, (dz, dy) in enumerate(CHIP_STEPS):
        origin = chip_at(2 - dz, ring - dy) * 2 + core
        rows = pl.ds(origin * blocks_dev, blocks_dev)
        for a, held in enumerate((keys, values)):
            sent[2 * n + a].wait_recv()
            copy = pltpu.make_async_remote_copy(
                src_ref=held.at[rows], dst_ref=held.at[rows],
                send_sem=relay_send.at[n, a], recv_sem=relay_recv.at[n, a],
                device_id=partner, device_id_type=MESH,
            )
            copy.start()
            relayed.append(copy)
    for step in range(1, members):
        row_copy(step).start()
    for copy in relayed:
        copy.wait_recv()
    for copy in here:
        copy.wait()

    scale = LOG2E * head_dim ** -0.5

    def result_copy(step):
        dz, dy, dc = step_offsets(step)
        block = member_at(dz, dy, dc)
        return pltpu.make_async_remote_copy(
            src_ref=done.at[block],
            dst_ref=result_ref.at[:, columns(me, width)],
            send_sem=out_send.at[block],
            recv_sem=out_recv.at[me],
            device_id=(behind, block),
            device_id_type=MESH,
        )

    def one_block(step, carry):
        dz, dy, dc = step_offsets(step)
        block = member_at(dz, dy, dc)

        @pl.when(step > 0)
        def _():
            result_copy(step - 1).start()
            for a in range(2):
                token_copy(step, a).wait_recv()
            row_copy(step).wait_recv()

        query_all, grad_all = head_query[block], head_grad[block]
        cuts = [slice(h * head_dim, (h + 1) * head_dim) for h in range(heads_here)]
        query = jnp.concatenate([query_all[:, cut] for cut in cuts], 0)
        grad = jnp.concatenate(
            [
                (grad_all[:, cut].astype(jnp.float32) * gates[h : h + 1, :]).astype(jnp.bfloat16)
                for h, cut in enumerate(cuts)
            ],
            0,
        )
        per_row = row_pack[block].T
        delta = jnp.concatenate([per_row[:, h : h + 1] for h in range(heads_here)], 0)
        log_total = jnp.concatenate([per_row[:, heads_here + h : heads_here + h + 1] for h in range(heads_here)], 0)

        def tile(t, total):
            picked = [picks_ref[chip, block, t * PICKS_A_TILE + i] for i in range(PICKS_A_TILE)]
            tile_keys = jnp.concatenate([keys[pick] for pick in picked], 0)
            tile_values = jnp.concatenate([values[pick] for pick in picked], 0)
            scores = lax.dot_general(query, tile_keys, CONTRACT_LAST, preferred_element_type=jnp.float32)
            grad_probs = lax.dot_general(grad, tile_values, CONTRACT_LAST, preferred_element_type=jnp.float32)
            probs = jnp.exp2(scores * scale - log_total)
            grad_scores = (probs * (grad_probs - delta)).astype(jnp.bfloat16)
            return total + jnp.dot(grad_scores, tile_keys, preferred_element_type=jnp.float32)

        total = lax.fori_loop(
            0, picks_count // PICKS_A_TILE, tile, jnp.zeros((heads_here * tokens, head_dim), jnp.float32)
        )
        for h, cut in enumerate(cuts):
            done[block, :, cut] = total[h * tokens : (h + 1) * tokens].astype(jnp.bfloat16)
        return carry

    lax.fori_loop(0, members, one_block, 0)
    result_copy(members - 1).start()

    for copy in sent:
        copy.wait_send()
    for copy in relayed:
        copy.wait_send()

    def drain(step, carry):
        for a in range(2):
            token_copy(step, a).wait_send()
        row_copy(step).wait_send()
        return carry

    lax.fori_loop(1, members, drain, 0)

    def settle(i, carry):
        copy = pltpu.make_async_remote_copy(
            src_ref=done.at[i],
            dst_ref=result_ref.at[:, columns(i, width)],
            send_sem=out_send.at[i],
            recv_sem=out_recv.at[i],
            device_id=(behind, i),
            device_id_type=MESH,
        )
        copy.wait_send()
        copy.wait_recv()
        return carry

    lax.fori_loop(0, members, settle, 0)


def shards(grad_out, queries, mem_out, row_total, gate_logit, mem_keys, mem_values, retrieved):
    members = lax.axis_size("seq")
    sections = lax.axis_size("section")
    tokens, full_width = grad_out.shape[1:]
    head_count = gate_logit.shape[1]
    head_dim = full_width // head_count
    heads_here = head_count // members
    width = heads_here * head_dim
    mem_dev = mem_keys.shape[1]
    blocks_dev = mem_dev // BLOCK
    mem_blocks = blocks_dev * members
    any_space = pl.BlockSpec(memory_space=pl.ANY)
    vmem = pl.BlockSpec(memory_space=pltpu.VMEM)
    dma = pltpu.SemaphoreType.DMA
    steps = len(CHIP_STEPS)
    result = pl.pallas_call(
        functools.partial(kernel, sections, members, heads_here, head_dim, retrieved.shape[3]),
        out_shape=jax.ShapeDtypeStruct((tokens, full_width), jnp.bfloat16),
        in_specs=[any_space, any_space, any_space, vmem, vmem, any_space, any_space,
                  pl.BlockSpec(memory_space=pltpu.SMEM)],
        out_specs=any_space,
        scratch_shapes=[
            pltpu.VMEM((mem_blocks, BLOCK, head_dim), jnp.bfloat16),
            pltpu.VMEM((mem_blocks, BLOCK, head_dim), jnp.bfloat16),
            pltpu.VMEM((members, tokens, width), jnp.bfloat16),
            pltpu.VMEM((members, tokens, width), jnp.bfloat16),
            pltpu.VMEM((members, 2 * heads_here, tokens), jnp.float32),
            pltpu.VMEM((members, 2 * heads_here, tokens), jnp.float32),
            pltpu.VMEM((8, head_dim), jnp.float32),
            pltpu.VMEM((members, tokens, width), jnp.bfloat16),
            pltpu.VMEM((tokens, full_width), jnp.bfloat16),
            pltpu.VMEM((tokens, full_width), jnp.bfloat16),
            dma((steps, 2)),
            dma((steps, 2)),
            dma((steps + 1, 2)),
            dma((steps + 1, 2)),
            dma((members, 3)),
            dma((members, 3)),
            dma((members,)),
            dma((members,)),
            dma((6,)),
        ],
        compiler_params=pltpu.CompilerParams(
            collective_id=0, has_side_effects=True, vmem_limit_bytes=60 * 1024 * 1024
        ),
        name="relay_attention_backward",
    )(
        grad_out[0],
        queries[0],
        mem_out[0],
        row_total[0],
        gate_logit,
        mem_keys[0].reshape(blocks_dev, BLOCK, mem_keys.shape[2]),
        mem_values[0].reshape(blocks_dev, BLOCK, mem_values.shape[2]),
        retrieved[0],
    )
    return result[None]


def solution(mesh):
    return jax.shard_map(
        shards,
        mesh=mesh,
        in_specs=(
            P("section", "seq", None),
            P("section", "seq", None),
            P("section", "seq", None),
            P("section", "seq", None),
            P("section", None),
            P("section", "seq", None),
            P("section", "seq", None),
            P("section", None, None, None),
        ),
        out_specs=P("section", "seq", None),
        check_vma=False,
    )
```

```python
import functools

import jax
import jax.numpy as jnp
from jax import lax
from jax.experimental import pallas as pl
from jax.experimental.pallas import tpu as pltpu
from jax.sharding import PartitionSpec as P

BLOCK = 128
PICKS_A_TILE = 16
AHEAD = 4
FORWARD_FROM = 10
SHIFT = 1
LOG2E = 1.4426950408889634
MESH = pl.DeviceIdType.MESH
CONTRACT_LAST = (((1,), (1,)), ((), ()))
CHIP_STEPS = ((1, 0), (0, 1), (0, 3), (1, 1), (0, 2), (1, 3), (1, 2))


def step_offsets(step, core):
    away = (step + 12) // 14
    turn = (step + 5 + SHIFT * core) % 7
    pair = turn // 2 + turn % 2
    along = pair + (pair // 2) * (1 - 2 * (pair % 2))
    return away * (1 - turn % 2), away * along, (1 - away) * step + away * ((step + 5) // 7 - 1)


def kernel(
    sections, members, heads_here, head_dim, picks_count,
    grad_ref, query_ref, out_in_ref, total_ref, gate_ref, key_ref, value_ref, picks_ref,
    result_ref,
    memory, head_rows, memory_send, rows_send, row_pack, row_send, gates, done, passed, own_grad, own_out,
    key_send, key_recv, relay_send, relay_recv, token_send, token_recv, pass_send, pass_recv, out_send, out_recv, local_sem, stage_sem,
):
    section = lax.axis_index("section")
    me = lax.axis_index("seq")
    chips = members // 2
    ring = chips // 2
    core = me % 2
    chip = me // 2
    high = chip // ring
    low = chip % ring
    width = heads_here * head_dim
    blocks_dev = key_ref.shape[0]
    behind = (section + sections - 1) % sections
    ahead = (section + 1) % sections
    half = sections // 2
    turned_out = 1 - (section % half + half - 1) // half
    turned_in = 1 - (ahead % half + half - 1) // half
    relay_to = (((high + turned_out) % 2) * ring + low) * 2 + core
    source_high = (high + turned_in) % 2
    source = (source_high * ring + low) * 2 + core

    def chip_at(dz, dy):
        return ((high + dz) % 2) * ring + (low + dy) % ring

    def member_at(dz, dy, dc):
        return chip_at(dz, dy) * 2 + (core + dc) % 2

    barrier = pltpu.get_barrier_semaphore()

    def greet(i, carry):
        pl.semaphore_signal(barrier, inc=1, device_id=(section, (me + i) % members), device_id_type=MESH)
        return carry

    lax.fori_loop(1, members, greet, 0)
    pl.semaphore_signal(barrier, inc=1, device_id=(ahead, source), device_id_type=MESH)

    def columns(index, size):
        return pl.ds(pl.multiple_of(index * size, size), size)

    own_rows = pl.ds(me * blocks_dev, blocks_dev)

    def gather_memory(target, a, slot):
        return pltpu.make_async_copy(
            (key_ref, value_ref)[a].at[:, :, columns(target, head_dim)], memory_send.at[target, a], slot
        )

    def gather_rows(target, a, slot):
        return pltpu.make_async_copy(
            (query_ref, grad_ref)[a].at[:, columns(target, width)], rows_send.at[target, a], slot
        )

    for target in range(chips):
        for a in range(2):
            gather_memory(target, a, stage_sem.at[target, a]).start()
    own_copies = [
        pltpu.make_async_copy(grad_ref, own_grad, local_sem.at[0]),
        pltpu.make_async_copy(out_in_ref, own_out, local_sem.at[1]),
    ]
    for copy in own_copies:
        copy.start()
    for target in range(members):
        for a in range(2):
            gather_rows(target, a, stage_sem.at[chips + target, a]).start()
    pl.semaphore_wait(barrier, members)
    for target in range(chips):
        for a in range(2):
            gather_memory(target, a, stage_sem.at[target, a]).wait()

    sent = []
    for n, (dz, dy) in enumerate(CHIP_STEPS):
        target = chip_at(dz, dy)
        copy = pltpu.make_async_remote_copy(
            src_ref=memory_send.at[target],
            dst_ref=memory.at[:, own_rows],
            send_sem=key_send.at[n],
            recv_sem=key_recv.at[n],
            device_id=(section, target * 2 + core),
            device_id_type=MESH,
        )
        copy.start()
        sent.append(copy)
    partner = (section, chip * 2 + 1 - core)
    here = [
        pltpu.make_async_copy(memory_send.at[chip], memory.at[:, own_rows], local_sem.at[2]),
        pltpu.make_async_copy(rows_send.at[me], head_rows.at[me], local_sem.at[3]),
    ]
    copy = pltpu.make_async_remote_copy(
        src_ref=memory_send.at[chip], dst_ref=memory.at[:, own_rows],
        send_sem=relay_send.at[len(CHIP_STEPS)], recv_sem=relay_recv.at[len(CHIP_STEPS)],
        device_id=partner, device_id_type=MESH,
    )
    copy.start()
    relayed = [copy]

    def token_target(step):
        dc = step_offsets(step, core)[2]
        dz, dy, dc = step_offsets(step, (core + dc) % 2)
        return member_at(2 - dz, ring - dy, dc)

    def token_copy(step):
        target = token_target(step)
        return pltpu.make_async_remote_copy(
            src_ref=rows_send.at[target],
            dst_ref=head_rows.at[me],
            send_sem=token_send.at[step, 0],
            recv_sem=token_recv.at[step, 0],
            device_id=(section, target),
            device_id_type=MESH,
        )

    def row_copy(step):
        target = token_target(step)
        return pltpu.make_async_remote_copy(
            src_ref=row_send.at[target],
            dst_ref=row_pack.at[me],
            send_sem=token_send.at[step, 1],
            recv_sem=token_recv.at[step, 1],
            device_id=(section, target),
            device_id_type=MESH,
        )

    for target in range(members):
        for a in range(2):
            gather_rows(target, a, stage_sem.at[chips + target, a]).wait()
    token_copy(1).start()
    for copy in here:
        copy.start()

    gate_row = 1.0 / (1.0 + jnp.exp(-gate_ref[...]))
    lanes = lax.broadcasted_iota(jnp.int32, gate_row.shape, 1)
    for h in range(heads_here):
        mine = jnp.sum(jnp.where(lanes == me * heads_here + h, gate_row, 0.0), axis=1, keepdims=True)
        gates[h : h + 1, :] = jnp.broadcast_to(mine, (1, head_dim))
    for copy in own_copies:
        copy.wait()
    tokens = own_grad.shape[0]
    log_total = jnp.log2(total_ref[...].astype(jnp.float32)) + 0.5 * 7.0
    lane = lax.broadcasted_iota(jnp.int32, (tokens, tokens), 1)
    packed = jnp.zeros((tokens, tokens), jnp.float32)
    for h in range(members * heads_here):
        cut = slice(h * head_dim, (h + 1) * head_dim)
        gated = (own_grad[:, cut].astype(jnp.float32) * gate_row[:, h : h + 1]).astype(jnp.bfloat16)
        delta = jnp.sum(gated.astype(jnp.float32) * own_out[:, cut].astype(jnp.float32), axis=1, keepdims=True)
        packed = jnp.where(lane == h, delta, packed)
    packed = packed.T
    for i in range(members):
        cut = slice(i * heads_here, (i + 1) * heads_here)
        row_send[i] = jnp.concatenate([packed[cut], log_total[cut]], 0)
    row_pack[me] = row_send[me]
    for step in range(1, members):
        row_copy(step).start()
    for step in range(2, AHEAD):
        token_copy(step).start()

    for n, (dz, dy) in enumerate(CHIP_STEPS):
        origin = chip_at(2 - dz, ring - dy) * 2 + core
        rows = pl.ds(origin * blocks_dev, blocks_dev)
        sent[n].wait_recv()
        copy = pltpu.make_async_remote_copy(
            src_ref=memory.at[:, rows], dst_ref=memory.at[:, rows],
            send_sem=relay_send.at[n], recv_sem=relay_recv.at[n],
            device_id=partner, device_id_type=MESH,
        )
        copy.start()
        relayed.append(copy)
    for copy in relayed:
        copy.wait_recv()
    for copy in here:
        copy.wait()

    scale = LOG2E * head_dim ** -0.5

    def pass_copy(step):
        return pltpu.make_async_remote_copy(
            src_ref=done.at[step],
            dst_ref=passed.at[step],
            send_sem=pass_send.at[step],
            recv_sem=pass_recv.at[step],
            device_id=(behind, relay_to),
            device_id_type=MESH,
        )

    def owner_of(step):
        dz, dy, dc = step_offsets(step, core)
        return (((source_high + dz) % 2) * ring + (low + dy) % ring) * 2 + (core + dc) % 2

    def result_copy(step):
        return pltpu.make_async_remote_copy(
            src_ref=passed.at[step],
            dst_ref=result_ref.at[:, columns(source, width)],
            send_sem=out_send.at[step],
            recv_sem=out_recv.at[source],
            device_id=(section, owner_of(step)),
            device_id_type=MESH,
        )

    def result_here(step):
        return pltpu.make_async_copy(passed.at[step], result_ref.at[:, columns(source, width)], local_sem.at[4])

    def forward(step, carry):
        owner = owner_of(step)
        pass_copy(step).wait_recv()

        @pl.when(owner != me)
        def _():
            result_copy(step).start()

        @pl.when(owner == me)
        def _():
            result_here(step).start()

        return carry

    def one_block(step, carry):
        dz, dy, dc = step_offsets(step, core)
        block = member_at(dz, dy, dc)

        @pl.when(step > 0)
        def _():
            pass_copy(step - 1).start()

        @pl.when(step < members - AHEAD)
        def _():
            token_copy(step + AHEAD).start()

        @pl.when(step > 0)
        def _():
            token_copy(step).wait_recv()
            row_copy(step).wait_recv()

        @pl.when(step >= FORWARD_FROM)
        def _():
            first = (step - FORWARD_FROM) * 2
            lax.fori_loop(first, first + 2, forward, 0)

        query_all, grad_all = head_rows[block, 0], head_rows[block, 1]
        cuts = [slice(h * head_dim, (h + 1) * head_dim) for h in range(heads_here)]
        query = jnp.concatenate([query_all[:, cut] for cut in cuts], 0)
        grad = jnp.concatenate(
            [
                (grad_all[:, cut].astype(jnp.float32) * gates[h : h + 1, :]).astype(jnp.bfloat16)
                for h, cut in enumerate(cuts)
            ],
            0,
        )
        per_row = row_pack[block].T
        delta = jnp.concatenate([per_row[:, h : h + 1] for h in range(heads_here)], 0)
        log_total = jnp.concatenate([per_row[:, heads_here + h : heads_here + h + 1] for h in range(heads_here)], 0)

        def tile(t, total):
            picked = [picks_ref[chip, block, t * PICKS_A_TILE + i] for i in range(PICKS_A_TILE)]
            tile_keys = jnp.concatenate([memory[0, pick] for pick in picked], 0)
            tile_values = jnp.concatenate([memory[1, pick] for pick in picked], 0)
            scores = lax.dot_general(query, tile_keys, CONTRACT_LAST, preferred_element_type=jnp.float32)
            grad_probs = lax.dot_general(grad, tile_values, CONTRACT_LAST, preferred_element_type=jnp.float32)
            probs = jnp.exp2(scores * scale - log_total)
            grad_scores = (probs * (grad_probs - delta)).astype(jnp.bfloat16)
            return total + jnp.dot(grad_scores, tile_keys, preferred_element_type=jnp.float32)

        total = lax.fori_loop(
            0, picks_count // PICKS_A_TILE, tile, jnp.zeros((heads_here * tokens, head_dim), jnp.float32)
        )
        for h, cut in enumerate(cuts):
            done[step, :, cut] = total[h * tokens : (h + 1) * tokens].astype(jnp.bfloat16)
        return carry

    lax.fori_loop(0, members, one_block, 0)
    pass_copy(members - 1).start()
    lax.fori_loop((members - FORWARD_FROM) * 2, members, forward, 0)

    for copy in sent:
        copy.wait_send()
    for copy in relayed:
        copy.wait_send()

    def drain(step, carry):
        token_copy(step).wait_send()
        row_copy(step).wait_send()
        return carry

    lax.fori_loop(1, members, drain, 0)

    def settle(step, carry):
        pass_copy(step).wait_send()

        @pl.when(owner_of(step) != me)
        def _():
            result_copy(step).wait_send()

        @pl.when(owner_of(step) == me)
        def _():
            result_here(step).wait()

        @pl.when(step != source)
        def _():
            pltpu.make_async_remote_copy(
                src_ref=passed.at[step],
                dst_ref=result_ref.at[:, columns(step, width)],
                send_sem=out_send.at[step],
                recv_sem=out_recv.at[step],
                device_id=partner,
                device_id_type=MESH,
            ).wait_recv()

        return carry

    lax.fori_loop(0, members, settle, 0)


def shards(grad_out, queries, mem_out, row_total, gate_logit, mem_keys, mem_values, retrieved):
    members = lax.axis_size("seq")
    sections = lax.axis_size("section")
    tokens, full_width = grad_out.shape[1:]
    head_count = gate_logit.shape[1]
    head_dim = full_width // head_count
    heads_here = head_count // members
    width = heads_here * head_dim
    mem_dev = mem_keys.shape[1]
    blocks_dev = mem_dev // BLOCK
    mem_blocks = blocks_dev * members
    any_space = pl.BlockSpec(memory_space=pl.ANY)
    vmem = pl.BlockSpec(memory_space=pltpu.VMEM)
    dma = pltpu.SemaphoreType.DMA
    steps = len(CHIP_STEPS)
    result = pl.pallas_call(
        functools.partial(kernel, sections, members, heads_here, head_dim, retrieved.shape[3]),
        out_shape=jax.ShapeDtypeStruct((tokens, full_width), jnp.bfloat16),
        in_specs=[any_space, any_space, any_space, vmem, vmem, any_space, any_space,
                  pl.BlockSpec(memory_space=pltpu.SMEM)],
        out_specs=any_space,
        scratch_shapes=[
            pltpu.VMEM((2, mem_blocks, BLOCK, head_dim), jnp.bfloat16),
            pltpu.VMEM((members, 2, tokens, width), jnp.bfloat16),
            pltpu.VMEM((members // 2, 2, blocks_dev, BLOCK, head_dim), jnp.bfloat16),
            pltpu.VMEM((members, 2, tokens, width), jnp.bfloat16),
            pltpu.VMEM((members, 2 * heads_here, tokens), jnp.float32),
            pltpu.VMEM((members, 2 * heads_here, tokens), jnp.float32),
            pltpu.VMEM((8, head_dim), jnp.float32),
            pltpu.VMEM((members, tokens, width), jnp.bfloat16),
            pltpu.VMEM((members, tokens, width), jnp.bfloat16),
            pltpu.VMEM((tokens, full_width), jnp.bfloat16),
            pltpu.VMEM((tokens, full_width), jnp.bfloat16),
            dma((steps,)),
            dma((steps,)),
            dma((steps + 1,)),
            dma((steps + 1,)),
            dma((members, 2)),
            dma((members, 2)),
            dma((members,)),
            dma((members,)),
            dma((members,)),
            dma((members,)),
            dma((5,)),
            dma((members // 2 + members, 2)),
        ],
        compiler_params=pltpu.CompilerParams(
            collective_id=0, has_side_effects=True, vmem_limit_bytes=60 * 1024 * 1024
        ),
        name="relay_attention_backward",
    )(
        grad_out[0],
        queries[0],
        mem_out[0],
        row_total[0].T,
        gate_logit,
        mem_keys[0].reshape(blocks_dev, BLOCK, mem_keys.shape[2]),
        mem_values[0].reshape(blocks_dev, BLOCK, mem_values.shape[2]),
        retrieved[0],
    )
    return result[None]


def solution(mesh):
    return jax.shard_map(
        shards,
        mesh=mesh,
        in_specs=(
            P("section", "seq", None),
            P("section", "seq", None),
            P("section", "seq", None),
            P("section", "seq", None),
            P("section", None),
            P("section", "seq", None),
            P("section", "seq", None),
            P("section", None, None, None),
        ),
        out_specs=P("section", "seq", None),
        check_vma=False,
    )
```

```python
import functools

import jax
import jax.numpy as jnp
from jax import lax
from jax.experimental import pallas as pl
from jax.experimental.pallas import tpu as pltpu
from jax.sharding import PartitionSpec as P

BLOCK = 128
PICKS_A_TILE = 16
AHEAD = 6
FORWARD_FROM = 9
SHIFT = 1
LOG2E = 1.4426950408889634
MESH = pl.DeviceIdType.MESH
CONTRACT_LAST = (((1,), (1,)), ((), ()))
CHIP_STEPS = ((1, 0), (0, 1), (0, 3), (1, 1), (0, 2), (1, 3), (1, 2))


def step_offsets(step, core):
    away = (step + 12) // 14
    turn = (step + 5 + SHIFT * core) % 7
    pair = turn // 2 + turn % 2
    along = pair + (pair // 2) * (1 - 2 * (pair % 2))
    return away * (1 - turn % 2), away * along, (1 - away) * step + away * ((step + 5) // 7 - 1)


def kernel(
    sections, members, heads_here, head_dim, picks_count,
    grad_ref, query_ref, out_in_ref, total_ref, gate_ref, key_ref, value_ref, picks_ref,
    result_ref,
    memory, head_rows, memory_send, rows_send, row_pack, row_send, gates, done, passed, own_grad, own_out,
    key_send, key_recv, relay_send, relay_recv, token_send, token_recv, pass_send, pass_recv, out_send, out_recv, local_sem, stage_sem,
):
    section = lax.axis_index("section")
    me = lax.axis_index("seq")
    chips = members // 2
    ring = chips // 2
    core = me % 2
    chip = me // 2
    high = chip // ring
    low = chip % ring
    width = heads_here * head_dim
    blocks_dev = key_ref.shape[0]
    behind = (section + sections - 1) % sections
    ahead = (section + 1) % sections
    half = sections // 2
    turned_out = 1 - (section % half + half - 1) // half
    turned_in = 1 - (ahead % half + half - 1) // half
    relay_to = (((high + turned_out) % 2) * ring + low) * 2 + core
    source_high = (high + turned_in) % 2
    source = (source_high * ring + low) * 2 + core

    def chip_at(dz, dy):
        return ((high + dz) % 2) * ring + (low + dy) % ring

    def member_at(dz, dy, dc):
        return chip_at(dz, dy) * 2 + (core + dc) % 2

    barrier = pltpu.get_barrier_semaphore()

    def greet(i, carry):
        pl.semaphore_signal(barrier, inc=1, device_id=(section, (me + i) % members), device_id_type=MESH)
        return carry

    lax.fori_loop(1, members, greet, 0)
    pl.semaphore_signal(barrier, inc=1, device_id=(ahead, source), device_id_type=MESH)

    def columns(index, size):
        return pl.ds(pl.multiple_of(index * size, size), size)

    own_rows = pl.ds(me * blocks_dev, blocks_dev)

    def gather_memory(target, a, slot):
        return pltpu.make_async_copy(
            (key_ref, value_ref)[a].at[:, :, columns(target, head_dim)], memory_send.at[target, a], slot
        )

    def gather_rows(target, a, slot):
        return pltpu.make_async_copy(
            (query_ref, grad_ref)[a].at[:, columns(target, width)], rows_send.at[target, a], slot
        )

    for target in range(chips):
        for a in range(2):
            gather_memory(target, a, stage_sem.at[target, a]).start()
    own_copies = [
        pltpu.make_async_copy(grad_ref, own_grad, local_sem.at[0]),
        pltpu.make_async_copy(out_in_ref, own_out, local_sem.at[1]),
    ]
    for copy in own_copies:
        copy.start()
    for target in range(members):
        for a in range(2):
            gather_rows(target, a, stage_sem.at[chips + target, a]).start()
    pl.semaphore_wait(barrier, members)
    for target in range(chips):
        for a in range(2):
            gather_memory(target, a, stage_sem.at[target, a]).wait()

    sent = []
    for n, (dz, dy) in enumerate(CHIP_STEPS):
        target = chip_at(dz, dy)
        copy = pltpu.make_async_remote_copy(
            src_ref=memory_send.at[target],
            dst_ref=memory.at[:, own_rows],
            send_sem=key_send.at[n],
            recv_sem=key_recv.at[n],
            device_id=(section, target * 2 + core),
            device_id_type=MESH,
        )
        copy.start()
        sent.append(copy)
    partner = (section, chip * 2 + 1 - core)
    here = [
        pltpu.make_async_copy(memory_send.at[chip], memory.at[:, own_rows], local_sem.at[2]),
        pltpu.make_async_copy(rows_send.at[me], head_rows.at[me], local_sem.at[3]),
    ]
    copy = pltpu.make_async_remote_copy(
        src_ref=memory_send.at[chip], dst_ref=memory.at[:, own_rows],
        send_sem=relay_send.at[len(CHIP_STEPS)], recv_sem=relay_recv.at[len(CHIP_STEPS)],
        device_id=partner, device_id_type=MESH,
    )
    copy.start()
    relayed = [copy]

    def token_target(step):
        dc = step_offsets(step, core)[2]
        dz, dy, dc = step_offsets(step, (core + dc) % 2)
        return member_at(2 - dz, ring - dy, dc)

    def token_copy(step):
        target = token_target(step)
        return pltpu.make_async_remote_copy(
            src_ref=rows_send.at[target],
            dst_ref=head_rows.at[me],
            send_sem=token_send.at[step, 0],
            recv_sem=token_recv.at[step, 0],
            device_id=(section, target),
            device_id_type=MESH,
        )

    def row_copy(step):
        target = token_target(step)
        return pltpu.make_async_remote_copy(
            src_ref=row_send.at[target],
            dst_ref=row_pack.at[me],
            send_sem=token_send.at[step, 1],
            recv_sem=token_recv.at[step, 1],
            device_id=(section, target),
            device_id_type=MESH,
        )

    for target in range(members):
        for a in range(2):
            gather_rows(target, a, stage_sem.at[chips + target, a]).wait()
    token_copy(1).start()
    for copy in here:
        copy.start()

    gate_row = 1.0 / (1.0 + jnp.exp(-gate_ref[...]))
    lanes = lax.broadcasted_iota(jnp.int32, gate_row.shape, 1)
    for h in range(heads_here):
        mine = jnp.sum(jnp.where(lanes == me * heads_here + h, gate_row, 0.0), axis=1, keepdims=True)
        gates[h : h + 1, :] = jnp.broadcast_to(mine, (1, head_dim))
    for copy in own_copies:
        copy.wait()
    tokens = own_grad.shape[0]
    log_total = jnp.log2(total_ref[...].astype(jnp.float32)) + 0.5 * 7.0
    lane = lax.broadcasted_iota(jnp.int32, (tokens, tokens), 1)
    packed = jnp.zeros((tokens, tokens), jnp.float32)
    for h in range(members * heads_here):
        cut = slice(h * head_dim, (h + 1) * head_dim)
        gated = (own_grad[:, cut].astype(jnp.float32) * gate_row[:, h : h + 1]).astype(jnp.bfloat16)
        delta = jnp.sum(gated.astype(jnp.float32) * own_out[:, cut].astype(jnp.float32), axis=1, keepdims=True)
        packed = jnp.where(lane == h, delta, packed)
    packed = packed.T
    for i in range(members):
        cut = slice(i * heads_here, (i + 1) * heads_here)
        row_send[i] = jnp.concatenate([packed[cut], log_total[cut]], 0)
    row_pack[me] = row_send[me]
    for step in range(1, members):
        row_copy(step).start()
    for step in range(2, AHEAD):
        token_copy(step).start()

    for n, (dz, dy) in enumerate(CHIP_STEPS):
        origin = chip_at(2 - dz, ring - dy) * 2 + core
        rows = pl.ds(origin * blocks_dev, blocks_dev)
        sent[n].wait_recv()
        copy = pltpu.make_async_remote_copy(
            src_ref=memory.at[:, rows], dst_ref=memory.at[:, rows],
            send_sem=relay_send.at[n], recv_sem=relay_recv.at[n],
            device_id=partner, device_id_type=MESH,
        )
        copy.start()
        relayed.append(copy)
    for copy in relayed:
        copy.wait_recv()
    for copy in here:
        copy.wait()

    scale = LOG2E * head_dim ** -0.5

    def pass_copy(step):
        return pltpu.make_async_remote_copy(
            src_ref=done.at[step],
            dst_ref=passed.at[step],
            send_sem=pass_send.at[step],
            recv_sem=pass_recv.at[step],
            device_id=(behind, relay_to),
            device_id_type=MESH,
        )

    def owner_of(step):
        dz, dy, dc = step_offsets(step, core)
        return (((source_high + dz) % 2) * ring + (low + dy) % ring) * 2 + (core + dc) % 2

    def result_copy(step):
        return pltpu.make_async_remote_copy(
            src_ref=passed.at[step],
            dst_ref=result_ref.at[:, columns(source, width)],
            send_sem=out_send.at[step],
            recv_sem=out_recv.at[source],
            device_id=(section, owner_of(step)),
            device_id_type=MESH,
        )

    def result_here(step):
        return pltpu.make_async_copy(passed.at[step], result_ref.at[:, columns(source, width)], local_sem.at[4])

    def forward(step, carry):
        owner = owner_of(step)
        pass_copy(step).wait_recv()

        @pl.when(owner != me)
        def _():
            result_copy(step).start()

        @pl.when(owner == me)
        def _():
            result_here(step).start()

        return carry

    def one_block(step, carry):
        dz, dy, dc = step_offsets(step, core)
        block = member_at(dz, dy, dc)

        @pl.when(step > 0)
        def _():
            pass_copy(step - 1).start()

        @pl.when(step < members - AHEAD)
        def _():
            token_copy(step + AHEAD).start()

        @pl.when(step > 0)
        def _():
            token_copy(step).wait_recv()
            row_copy(step).wait_recv()

        @pl.when(step >= FORWARD_FROM)
        def _():
            first = (step - FORWARD_FROM) * 2
            lax.fori_loop(first, first + 2, forward, 0)

        query_all, grad_all = head_rows[block, 0], head_rows[block, 1]
        cuts = [slice(h * head_dim, (h + 1) * head_dim) for h in range(heads_here)]
        query = jnp.concatenate([query_all[:, cut] for cut in cuts], 0)
        grad = jnp.concatenate(
            [
                (grad_all[:, cut].astype(jnp.float32) * gates[h : h + 1, :]).astype(jnp.bfloat16)
                for h, cut in enumerate(cuts)
            ],
            0,
        )
        per_row = row_pack[block].T
        delta = jnp.concatenate([per_row[:, h : h + 1] for h in range(heads_here)], 0)
        log_total = jnp.concatenate([per_row[:, heads_here + h : heads_here + h + 1] for h in range(heads_here)], 0)

        def tile(t, total):
            picked = [picks_ref[chip, block, t * PICKS_A_TILE + i] for i in range(PICKS_A_TILE)]
            tile_keys = jnp.concatenate([memory[0, pick] for pick in picked], 0)
            tile_values = jnp.concatenate([memory[1, pick] for pick in picked], 0)
            scores = lax.dot_general(query, tile_keys, CONTRACT_LAST, preferred_element_type=jnp.float32)
            grad_probs = lax.dot_general(grad, tile_values, CONTRACT_LAST, preferred_element_type=jnp.float32)
            probs = jnp.exp2(scores * scale - log_total)
            grad_scores = (probs * (grad_probs - delta)).astype(jnp.bfloat16)
            return total + jnp.dot(grad_scores, tile_keys, preferred_element_type=jnp.float32)

        total = lax.fori_loop(
            0, picks_count // PICKS_A_TILE, tile, jnp.zeros((heads_here * tokens, head_dim), jnp.float32)
        )
        for h, cut in enumerate(cuts):
            done[step, :, cut] = total[h * tokens : (h + 1) * tokens].astype(jnp.bfloat16)
        return carry

    lax.fori_loop(0, members, one_block, 0)
    pass_copy(members - 1).start()
    lax.fori_loop((members - FORWARD_FROM) * 2, members, forward, 0)

    for copy in sent:
        copy.wait_send()
    for copy in relayed:
        copy.wait_send()

    def drain(step, carry):
        token_copy(step).wait_send()
        row_copy(step).wait_send()
        return carry

    lax.fori_loop(1, members, drain, 0)

    def settle(step, carry):
        pass_copy(step).wait_send()

        @pl.when(owner_of(step) != me)
        def _():
            result_copy(step).wait_send()

        @pl.when(owner_of(step) == me)
        def _():
            result_here(step).wait()

        @pl.when(step != source)
        def _():
            pltpu.make_async_remote_copy(
                src_ref=passed.at[step],
                dst_ref=result_ref.at[:, columns(step, width)],
                send_sem=out_send.at[step],
                recv_sem=out_recv.at[step],
                device_id=partner,
                device_id_type=MESH,
            ).wait_recv()

        return carry

    lax.fori_loop(0, members, settle, 0)


def shards(grad_out, queries, mem_out, row_total, gate_logit, mem_keys, mem_values, retrieved):
    members = lax.axis_size("seq")
    sections = lax.axis_size("section")
    tokens, full_width = grad_out.shape[1:]
    head_count = gate_logit.shape[1]
    head_dim = full_width // head_count
    heads_here = head_count // members
    width = heads_here * head_dim
    mem_dev = mem_keys.shape[1]
    blocks_dev = mem_dev // BLOCK
    mem_blocks = blocks_dev * members
    any_space = pl.BlockSpec(memory_space=pl.ANY)
    vmem = pl.BlockSpec(memory_space=pltpu.VMEM)
    dma = pltpu.SemaphoreType.DMA
    steps = len(CHIP_STEPS)
    result = pl.pallas_call(
        functools.partial(kernel, sections, members, heads_here, head_dim, retrieved.shape[3]),
        out_shape=jax.ShapeDtypeStruct((tokens, full_width), jnp.bfloat16),
        in_specs=[any_space, any_space, any_space, vmem, vmem, any_space, any_space,
                  pl.BlockSpec(memory_space=pltpu.SMEM)],
        out_specs=any_space,
        scratch_shapes=[
            pltpu.VMEM((2, mem_blocks, BLOCK, head_dim), jnp.bfloat16),
            pltpu.VMEM((members, 2, tokens, width), jnp.bfloat16),
            pltpu.VMEM((members // 2, 2, blocks_dev, BLOCK, head_dim), jnp.bfloat16),
            pltpu.VMEM((members, 2, tokens, width), jnp.bfloat16),
            pltpu.VMEM((members, 2 * heads_here, tokens), jnp.float32),
            pltpu.VMEM((members, 2 * heads_here, tokens), jnp.float32),
            pltpu.VMEM((8, head_dim), jnp.float32),
            pltpu.VMEM((members, tokens, width), jnp.bfloat16),
            pltpu.VMEM((members, tokens, width), jnp.bfloat16),
            pltpu.VMEM((tokens, full_width), jnp.bfloat16),
            pltpu.VMEM((tokens, full_width), jnp.bfloat16),
            dma((steps,)),
            dma((steps,)),
            dma((steps + 1,)),
            dma((steps + 1,)),
            dma((members, 2)),
            dma((members, 2)),
            dma((members,)),
            dma((members,)),
            dma((members,)),
            dma((members,)),
            dma((5,)),
            dma((members // 2 + members, 2)),
        ],
        compiler_params=pltpu.CompilerParams(
            collective_id=0, has_side_effects=True, vmem_limit_bytes=60 * 1024 * 1024
        ),
        name="relay_attention_backward",
    )(
        grad_out[0],
        queries[0],
        mem_out[0],
        row_total[0].T,
        gate_logit,
        mem_keys[0].reshape(blocks_dev, BLOCK, mem_keys.shape[2]),
        mem_values[0].reshape(blocks_dev, BLOCK, mem_values.shape[2]),
        retrieved[0],
    )
    return result[None]


def solution(mesh):
    return jax.shard_map(
        shards,
        mesh=mesh,
        in_specs=(
            P("section", "seq", None),
            P("section", "seq", None),
            P("section", "seq", None),
            P("section", "seq", None),
            P("section", None),
            P("section", "seq", None),
            P("section", "seq", None),
            P("section", None, None, None),
        ),
        out_specs=P("section", "seq", None),
        check_vma=False,
    )
```
